128 devices in a mesh: expert: 2 (over z_lo), tensor: 64 (over z_hi, x, y, core).
Axes of the slice: x: 4, y: 4, z: 4 (z_hi: 2, z_lo: 2; z = z_hi * 2 + z_lo), core: 2. Of those that a mesh axis runs over, the one named last changes fastest.
Arguments:
- tokens: bfloat16 [512, 6144], P(('expert', 'tensor')), may hold values from -6 to 6
- gate_weights: bfloat16 [512, 2], P(('expert', 'tensor')), may hold values from 0.19921875 to 1
- expert_ids: int32 [512, 2], P(('expert', 'tensor')), may hold values from 0 to 3, all different within a row; in each aligned block of 512 rows (0 to 511, 512 to 1023, ...) at most 384 rows name the same one
- w_gate: bfloat16 [4, 6144, 16384], P('expert', None, 'tensor'), may hold values from -0.078125 to 0.078125
- w_up: bfloat16 [4, 6144, 16384], P('expert', None, 'tensor'), may hold values from -0.078125 to 0.078125
- w_down: bfloat16 [4, 16384, 6144], P('expert', 'tensor'), may hold values from -0.046875 to 0.046875
Outputs:
- mixed: bfloat16 [512, 6144], P(('expert', 'tensor'))
The draws below stay inside these ranges and needn't reach their ends.
Inputs may be any that keep to these rules, and one draw needn't show every extreme that they name: `expert_ids`: the 2 ids of a token differ; every expert is named by at most 384 tokens, a bound that some block reaches.
All inputs are finite; a program needn't handle non-finite values.
Results may differ from the reference program's by a relative error of at most 0.0049.
Values may be sent and summed in bfloat16 or wider, within the bound.
A program may use at most 192 MiB of HBM per device.

```python
import math
import jax
import jax.numpy as jnp
import numpy as np

D = 6144
FF = 16384
TOP = 2
EXPERTS = 4
TOKENS = 512
CAP = 384


def block_levels(own_key, shape, pieces, low, high):
    def one(dim, parts):
        heights = jax.random.uniform(jax.random.fold_in(jax.random.fold_in(own_key, 6), dim), (parts,), jnp.float32, low / len(pieces), high / len(pieces))
        return jnp.repeat(jnp.exp(heights), shape[dim] // parts).reshape((-1,) + (1,) * (len(shape) - dim - 1))

    factor_of = one(*pieces[0])
    for cut in pieces[1:]:
        factor_of = factor_of * one(*cut)
    return factor_of


def shared_out(rng, own, number, rows, count, top, bound, slope):
    order = jax.random.permutation(rng, count)
    heavy_load, ordinary = portions_of(count, rows * top, bound, slope, True), portions_of(count, rows * top, bound, slope, False)
    places = jnp.arange(count)

    def named(sizes, turn):
        used = int((sizes > 0).sum())
        fixed = max(1, used // 4)
        shifted = fixed + (places - fixed + turn * (used - fixed)) % max(1, count - fixed)
        return jnp.zeros((count,), jnp.int32).at[order[jnp.where(places < fixed, places, shifted)]].set(jnp.asarray(sizes, jnp.int32))

    sizes = jnp.where(number % 4 == 0, named(heavy_load, number // 4), named(ordinary, number - number // 4 - 1))
    mixed = jax.random.permutation(jax.random.fold_in(own, 3), count)
    donor, sink = mixed[0:count // 2 * 2:2], mixed[1:count // 2 * 2:2]
    margin = jnp.minimum(sizes[donor] - 1, bound - sizes[sink]) // 2
    margin = jnp.where((donor == order[0]) | (sink == order[0]) | (sizes[sink] == 0), 0, jnp.maximum(margin, 0))
    shifted = jax.random.randint(jax.random.fold_in(own, 4), (count // 2,), 0, 1 << 20) % (margin + 1)
    sizes = sizes.at[donor].add(-shifted).at[sink].add(shifted)
    labels = jnp.searchsorted(jnp.cumsum(sizes), jnp.arange(rows * top), side="right").astype(jnp.int32)
    listing = labels.reshape(top, rows).T
    listing = listing[jax.random.permutation(jax.random.fold_in(own, 1), rows)]
    turn = jax.random.randint(jax.random.fold_in(own, 2), (rows, 1), 0, top)
    return jnp.take_along_axis(listing, (jnp.arange(top)[None, :] + turn) % top, axis=1)


def portions_of(number_of, total, limit, slope, full):
    loads = [(1 << 20) // math.isqrt(grade ** slope) + 1 for grade in range(1, number_of + 1)]
    largest = limit if full else min(limit, max(-(-total // number_of), total * loads[0] // sum(loads)))
    least = 1 if total - largest >= number_of - 1 else 0
    counts, surplus = [largest] + [least] * (number_of - 1), total - largest - least * (number_of - 1)
    while surplus > 0:
        movable = [i for i in range(1, number_of) if counts[i] < largest] or [i for i in range(1, number_of) if counts[i] < limit]
        pool, remaining = sum([loads[i] for i in movable]), surplus
        for i in movable:
            addition = min(limit - counts[i], max(1, remaining * loads[i] // pool), surplus)
            counts[i] = counts[i] + addition
            surplus = surplus - addition
    return np.array(counts)


def noise(rng, dims, scale, reach, split=(), kind=jnp.bfloat16):
    loudness = block_levels(rng, dims, split, -0.22, 0.18) if split else 1.0
    array = jax.random.normal(rng, dims, jnp.float32) * scale * loudness
    return jnp.minimum(jnp.maximum(array, -reach), reach).astype(kind)


def setup_inputs(seed: int = 0) -> dict:
    arg_keys = jax.random.split(jax.random.key(seed), 7)
    tokens = noise(arg_keys[0], (TOKENS, D), 1.0, 6.0, ((0, 128),))
    gate_weights = jnp.clip(0.19921875 + 0.80078125 * jax.random.uniform(arg_keys[1], (TOKENS, TOP), jnp.float32) ** block_levels(arg_keys[1], (TOKENS, TOP), ((0, 128),), -0.2, 0.2), 0.19921875, 1.0).astype(jnp.bfloat16)
    expert_ids_keys = jax.random.split(jax.random.fold_in(arg_keys[2], 1), TOKENS // TOKENS)
    expert_ids_turns = jax.random.permutation(jax.random.fold_in(arg_keys[2], 3), TOKENS // TOKENS)
    expert_ids = jax.vmap(lambda own, number: shared_out(jax.random.fold_in(arg_keys[2], 2), own, number, TOKENS, EXPERTS, TOP, CAP, 2))(expert_ids_keys, expert_ids_turns).reshape((TOKENS, TOP))
    w_gate = noise(arg_keys[3], (EXPERTS, D, FF), D ** -0.5, 0.078125, ((0, 2), (2, 64)))
    w_up = noise(arg_keys[4], (EXPERTS, D, FF), D ** -0.5, 0.078125, ((0, 2), (2, 64)))
    w_down = noise(arg_keys[5], (EXPERTS, FF, D), FF ** -0.5, 0.046875, ((0, 2), (1, 64)))
    return {"tokens": tokens, "gate_weights": gate_weights, "expert_ids": expert_ids, "w_gate": w_gate, "w_up": w_up, "w_down": w_down}


def routing_lists(expert_ids, gate_weights, expert, capacity):
    matches = expert_ids == expert
    chosen = jnp.any(matches, axis=1)
    weight = jnp.sum(jnp.where(matches, gate_weights.astype(jnp.float32), jnp.float32(0.0)), axis=1)
    ranking = jnp.cumsum(chosen.astype(jnp.int32)) - 1
    target = jnp.where(chosen, ranking, capacity).astype(jnp.int32)
    token_count = expert_ids.shape[0]
    slot_tok = jnp.full((capacity,), token_count, jnp.int32).at[target].set(
        jnp.arange(token_count, dtype=jnp.int32), mode="drop")
    slot_gate = jnp.zeros((capacity,), jnp.float32).at[target].set(weight, mode="drop")
    return slot_tok, slot_gate


def reference(tokens, gate_weights, expert_ids, w_gate, w_up, w_down):
    summed = jnp.zeros((TOKENS, D), jnp.float32)
    for expert in range(EXPERTS):
        slot_tok, slot_gate = routing_lists(expert_ids, gate_weights, expert, CAP)
        slot_rows = tokens[jnp.minimum(slot_tok, TOKENS - 1)]
        gate_proj = jnp.dot(slot_rows, w_gate[expert], preferred_element_type=jnp.float32)
        up_proj = jnp.dot(slot_rows, w_up[expert], preferred_element_type=jnp.float32)
        hidden = (jax.nn.silu(gate_proj) * up_proj).astype(jnp.bfloat16)
        expert_out = jnp.dot(hidden, w_down[expert], preferred_element_type=jnp.float32)
        summed = summed.at[slot_tok].add(expert_out * slot_gate[:, None], mode="drop")
    return summed.astype(jnp.bfloat16)
```

```python
import functools

import jax
import jax.numpy as jnp
from jax import lax
from jax.experimental import pallas as pl
from jax.experimental.pallas import tpu as pltpu
from jax.sharding import PartitionSpec as P

MESH = pl.DeviceIdType.MESH
BF = jnp.bfloat16
F32 = jnp.float32
ORDER = ((0, 1, 2), (1, 2, 0), (2, 0, 1))
PART = 1024
HALF = 3 * PART
GATE = 128
WIDE = HALF + GATE
START = (0, PART + GATE, 2 * PART + GATE)
CUT = (((0, 640), (640, 512)), ((1152, 512), (1664, 512)), ((2176, 512), (2688, 512)))
WHOLE = ((0, 1152), (1152, 1024), (2176, 1024))


def kernel(tok, ids, gts, wg, wu, wd, out, x_all, st, wgs, wus, wds, xs, acc, hid, own, own16, sp, rp,
           ma, ra, ta, ta16, mb, rb, tb, mc, rc, sd, rd,
           lsem, wsem, s0, r0, ags, agr, fs, fr, ps, pr, rss, rsr, ds, dr):
    e = lax.axis_index("expert")
    t = lax.axis_index("tensor")
    core = lax.rem(t, 2)
    pos = (lax.rem(lax.div(t, 8), 4), lax.rem(lax.div(t, 2), 4), lax.div(t, 32) * 2 + e)
    other = 1 - core

    def device(axis, step):
        at = list(pos)
        at[axis] = lax.rem(at[axis] + step + 4, 4)
        return (lax.rem(at[2], 2), lax.div(at[2], 2) * 32 + at[0] * 8 + at[1] * 2 + core)

    partner = (e, t + 1 - 2 * core)
    right = [device(a, 1) for a in range(3)]
    left = [device(a, -1) for a in range(3)]

    here = (pos[2], pos[1], pos[0], core)
    local = []
    mine = x_all.at[(core, *here)]
    for h, ref in enumerate((mine, st)):
        half = (core, other)[h]
        for i, (src, dst, n) in enumerate(((0, 0, PART), (PART, PART + GATE, 2 * PART))):
            c = pltpu.make_async_copy(
                tok.at[:, pl.ds(pl.multiple_of(half * HALF + src, PART), n)],
                ref.at[:, pl.ds(dst, n)], lsem.at[h, i])
            c.start()
            local.append(c)
    weights = []
    for i, (src, dst) in enumerate(((wg, wgs), (wu, wus), (wd, wds))):
        c = pltpu.make_async_copy(src, dst, wsem.at[i])
        c.start()
        weights.append(c)

    barrier = pltpu.get_barrier_semaphore()
    for d in [partner] + right + left:
        pl.semaphore_signal(barrier, inc=1, device_id=d, device_id_type=MESH)

    lane = lax.broadcasted_iota(jnp.int32, (4, GATE), 1)
    table = jnp.zeros((4, GATE), F32)
    for j in range(2):
        table += jnp.where(ids[:, j:j + 1] == lane, gts[:, j:j + 1].astype(F32), 0.0)
    mine[:, pl.ds(PART, GATE)] = table.astype(BF)
    st[:, pl.ds(PART, GATE)] = table.astype(BF)

    for c in local:
        c.wait()
    pl.semaphore_wait(barrier, 7)

    sent = []

    def send(src, dst, ssem, rsem, dev):
        c = pltpu.make_async_remote_copy(src_ref=src, dst_ref=dst, send_sem=ssem, recv_sem=rsem,
                                         device_id=dev, device_id_type=MESH)
        c.start()
        sent.append(c)
        return c

    c = send(st, x_all.at[(other, *here)], s0, r0, partner)
    c.wait_recv()

    def block(o, s, q, cols):
        at = []
        for axis in (2, 1, 0):
            if axis == ORDER[o][s]:
                at.append(q)
            elif axis in ORDER[o][:s]:
                at.append(slice(None))
            else:
                at.append(pos[axis])
        return x_all.at[(core, *at, slice(None), slice(None), pl.ds(*cols))]

    def near(o, s, step):
        return lax.rem(pos[ORDER[o][s]] + step + 4, 4)

    def gather(o, s, k, ref, dev):
        return send(ref, ref, ags.at[s, o, k], agr.at[s, o, k], dev)

    passed = {}

    def hand(o, j, step):
        ref = block(o, 2, near(o, 2, step), WHOLE[o])
        passed[o, j] = send(ref, ref, fs.at[o, j], fr.at[o, j], partner)

    for s in range(3):
        moves = {}
        for o in range(3):
            a = ORDER[o][s]
            me = near(o, s, 0)
            moves[o, 0] = gather(o, s, 0, block(o, s, me, CUT[o][0]), right[a])
            moves[o, 2] = gather(o, s, 2, block(o, s, me, CUT[o][1]), left[a])
            moves[o, 1] = gather(o, s, 1, block(o, s, me, CUT[o][1]), right[a])
            moves[o, 3] = gather(o, s, 3, block(o, s, me, CUT[o][0]), left[a])
        if s == 2:
            for o in range(3):
                hand(o, 0, 0)
        for o in range(3):
            a = ORDER[o][s]
            moves[o, 0].wait_recv()
            moves[o, 4] = gather(o, s, 4, block(o, s, near(o, s, -1), CUT[o][0]), right[a])
            moves[o, 2].wait_recv()
            moves[o, 5] = gather(o, s, 5, block(o, s, near(o, s, 1), CUT[o][1]), left[a])
        if s < 2:
            for o in range(3):
                for k in (1, 3, 4, 5):
                    moves[o, k].wait_recv()
        else:
            for o in range(3):
                moves[o, 1].wait_recv()
                hand(o, 1, -1)
                moves[o, 3].wait_recv()
                hand(o, 2, 1)
            for o in range(3):
                moves[o, 4].wait_recv()
                moves[o, 5].wait_recv()
                hand(o, 3, 2)

    for c in weights:
        c.wait()
    for turn, h in enumerate((core, other)):
        for o in range(3):
            if turn == 1:
                for j in range(4):
                    passed[o, j].wait_recv()
            for z in range(4):
                xs[pl.ds(z * 128, 128), :] = x_all[
                    h, z, :, :, :, :, pl.ds(START[o], PART)].reshape(128, PART)
            first = turn == 0 and o == 0

            def project(k, _):
                for m, w in ((0, wgs), (1, wus)):
                    r = jnp.dot(xs[...], w[k, h * 3 + o], preferred_element_type=F32)
                    acc[k, m] = r if first else acc[k, m] + r
                return 0

            lax.fori_loop(0, 2, project, 0)

    table = x_all[core, :, :, :, :, :, pl.ds(PART, GATE)].reshape(512, GATE).astype(F32)
    lane = lax.broadcasted_iota(jnp.int32, (512, GATE), 1)
    for k in range(2):
        g = jnp.sum(jnp.where(lane == 2 * e + k, table, 0.0), axis=1, keepdims=True)
        v = acc[k, 0]
        hid[:, k * 256:(k + 1) * 256] = (v / (1.0 + jnp.exp(-v)) * acc[k, 1] * g).astype(BF)

    def down(h, o, n):
        cols = pl.multiple_of(h * HALF + o * PART + n * 256, 256)
        r = jnp.dot(hid[...], wds[:, pl.ds(cols, 256)], preferred_element_type=F32)
        return pl.ds(pl.multiple_of(n * 256, 256), 256), r.reshape(4, 4, 4, 8, 256)

    pair = {}
    for o in range(3):
        def give(n, _):
            at, r = down(other, o, n)
            sp[o, :, :, :, :, at] = r.astype(BF)
            return 0

        lax.fori_loop(0, 4, give, 0)
        pair[o] = send(sp.at[o], rp.at[o], ps.at[o], pr.at[o], partner)

    moves = {}

    def reduce(s, o, k, src, dst, dev):
        moves[s, o, k] = send(src, dst, rss.at[s, o, k], rsr.at[s, o, k], dev)

    LOW, HIGH = pl.ds(0, 512), pl.ds(512, 512)

    def start(s, o, piece, recv):
        a = ORDER[o][2 - s]
        n = lambda step: near(o, 2 - s, step)
        reduce(s, o, 0, piece(o, n(2), LOW), recv.at[o, 0], right[a])
        reduce(s, o, 1, piece(o, n(2), HIGH), recv.at[o, 1], left[a])
        reduce(s, o, 2, piece(o, n(1), HIGH), recv.at[o, 2], right[a])
        reduce(s, o, 3, piece(o, n(-1), LOW), recv.at[o, 3], left[a])

    def merge(s, o, piece, recv, buf):
        a = ORDER[o][2 - s]
        n = lambda step: near(o, 2 - s, step)
        for k, step, cols, dev in ((0, 1, LOW, right[a]), (1, -1, HIGH, left[a])):
            moves[s, o, k].wait_recv()
            buf[o, k] = (piece(o, n(step), cols)[...] + recv[o, k].astype(F32)).astype(buf.dtype)
            reduce(s, o, 4 + k, buf.at[o, k], recv.at[o, 4 + k], dev)

    def final(s, o, piece, recv, put):
        me = near(o, 2 - s, 0)
        for cols, ks in ((LOW, (3, 4)), (HIGH, (2, 5))):
            r = piece(o, me, cols)[...]
            for k in ks:
                moves[s, o, k].wait_recv()
                r = r + recv[o, k].astype(F32)
            put(o, cols, r)

    def at_a(ref):
        def piece(o, q, cols):
            at = [q if axis == ORDER[o][2] else slice(None) for axis in (2, 1, 0)]
            return ref.at[(o, *at, slice(None), cols)]
        return piece

    def at_b(ref):
        def piece(o, q, cols):
            at = [q if axis == ORDER[o][1] else slice(None) for axis in (2, 1, 0) if axis != ORDER[o][2]]
            return ref.at[(o, *at, slice(None), cols)]
        return piece

    def at_c(ref):
        return lambda o, q, cols: ref.at[o, q, :, cols]

    for o in range(3):
        pair[o].wait_recv()

        def keep(n, _):
            at, r = down(core, o, n)
            r = r + rp[o, :, :, :, :, at].astype(F32)
            own[o, :, :, :, :, at] = r
            own16[o, :, :, :, :, at] = r.astype(BF)
            return 0

        lax.fori_loop(0, 4, keep, 0)
        start(0, o, at_a(own16), ra)
    for o in range(3):
        merge(0, o, at_a(own), ra, ma)

    def put_a(o, cols, r):
        ta[o, :, :, :, cols] = r
        ta16[o, :, :, :, cols] = r.astype(BF)

    for o in range(3):
        final(0, o, at_a(own), ra, put_a)
        start(1, o, at_b(ta16), rb)
    for o in range(3):
        merge(1, o, at_b(ta), rb, mb)

    def put_b(o, cols, r):
        tb[o, :, :, cols] = r

    for o in range(3):
        final(1, o, at_b(ta), rb, put_b)
        start(2, o, at_c(tb), rc)
    for o in range(3):
        merge(2, o, at_c(tb), rc, mc)

    def put_c(o, cols, r):
        at = pl.ds(o * PART + cols.start, cols.size)
        sd[:, at] = jnp.where(core == 0, r[4:8], r[0:4])
        to = pl.multiple_of(core * HALF + o * PART + cols.start, 512)
        out[:, pl.ds(to, cols.size)] = jnp.where(core == 0, r[0:4], r[4:8]).astype(BF)

    for o in range(3):
        final(2, o, at_c(tb), rc, put_c)
    c = send(sd, rd, ds, dr, partner)
    c.wait_recv()
    out[:, pl.ds(pl.multiple_of(other * HALF, HALF), HALF)] = rd[...].astype(BF)
    for c in sent:
        c.wait_send()


def shards(tokens, gate_weights, expert_ids, w_gate, w_up, w_down):
    anyspace = pl.BlockSpec(memory_space=pl.ANY)
    vmem = pl.BlockSpec(memory_space=pltpu.VMEM)
    dma = pltpu.SemaphoreType.DMA
    return pl.pallas_call(
        kernel,
        out_shape=jax.ShapeDtypeStruct((4, 2 * HALF), BF),
        in_specs=[anyspace, vmem, vmem, anyspace, anyspace, anyspace],
        out_specs=vmem,
        scratch_shapes=[
            pltpu.VMEM((2, 4, 4, 4, 2, 4, WIDE), BF),
            pltpu.VMEM((4, WIDE), BF),
            pltpu.VMEM((2, 6, PART, 256), BF),
            pltpu.VMEM((2, 6, PART, 256), BF),
            pltpu.VMEM((512, 2 * HALF), BF),
            pltpu.VMEM((512, PART), BF),
            pltpu.VMEM((2, 2, 512, 256), F32),
            pltpu.VMEM((512, 512), BF),
            pltpu.VMEM((3, 4, 4, 4, 8, PART), F32),
            pltpu.VMEM((3, 4, 4, 4, 8, PART), BF),
            pltpu.VMEM((3, 4, 4, 4, 8, PART), BF),
            pltpu.VMEM((3, 4, 4, 4, 8, PART), BF),
            pltpu.VMEM((3, 2, 4, 4, 8, 512), BF),
            pltpu.VMEM((3, 6, 4, 4, 8, 512), BF),
            pltpu.VMEM((3, 4, 4, 8, PART), F32),
            pltpu.VMEM((3, 4, 4, 8, PART), BF),
            pltpu.VMEM((3, 2, 4, 8, 512), BF),
            pltpu.VMEM((3, 6, 4, 8, 512), BF),
            pltpu.VMEM((3, 4, 8, PART), F32),
            pltpu.VMEM((3, 2, 8, 512), F32),
            pltpu.VMEM((3, 6, 8, 512), F32),
            pltpu.VMEM((4, HALF), F32),
            pltpu.VMEM((4, HALF), F32),
            dma((2, 2)), dma((3,)), dma, dma, dma((3, 3, 6)), dma((3, 3, 6)), dma((3, 4)), dma((3, 4)),
            dma((3,)), dma((3,)), dma((3, 3, 6)), dma((3, 3, 6)), dma, dma,
        ],
        compiler_params=pltpu.CompilerParams(
            collective_id=0, has_side_effects=True, vmem_limit_bytes=67043328),
        name="moe",
    )(tokens, expert_ids, gate_weights, w_gate.reshape(2, 6, PART, 256), w_up.reshape(2, 6, PART, 256),
      w_down.reshape(512, 2 * HALF))


def solution(mesh):
    rows = P(("expert", "tensor"), None)
    return jax.shard_map(
        shards, mesh=mesh,
        in_specs=(rows, rows, rows, P("expert", None, "tensor"), P("expert", None, "tensor"),
                  P("expert", "tensor", None)),
        out_specs=rows, check_vma=False)
```

```python
import functools

import jax
import jax.numpy as jnp
from jax import lax
from jax.experimental import pallas as pl
from jax.experimental.pallas import tpu as pltpu
from jax.sharding import PartitionSpec as P

MESH = pl.DeviceIdType.MESH
BF = jnp.bfloat16
F32 = jnp.float32
ORDER = ((0, 1, 2), (1, 2, 0), (2, 0, 1))
PART = 1024
HALF = 3 * PART
GATE = 128
WIDE = HALF + GATE
STEPS = (1, -1, 2)
START = (0, PART + GATE, 2 * PART + GATE)
CUT = (((0, 640), (640, 512)), ((1152, 512), (1664, 512)), ((2176, 512), (2688, 512)))
WHOLE = ((0, 1152), (1152, 1024), (2176, 1024))


def kernel(tok, ids, gts, wg, wu, wd, out, x_all, st, idv, gtv, wgs, wus, wds, xs, acc, hid, own, own16,
           sp, rp, ma, ra, ta, tb16, rb, tb, rc, sd, rd,
           lsem, wsem, s0, r0, a1s, a1r, a2s, a2r, a3s, a3r, fs, fr, ps, pr, b1s, b1r, b2s, b2r, b3s, b3r,
           ds, dr):
    e = lax.axis_index("expert")
    t = lax.axis_index("tensor")
    core = lax.rem(t, 2)
    pos = (lax.rem(lax.div(t, 8), 4), lax.rem(lax.div(t, 2), 4), lax.div(t, 32) * 2 + e)
    other = 1 - core

    def near(axis, step):
        return lax.rem(pos[axis] + step + 4, 4)

    def device(axis, step):
        at = list(pos)
        at[axis] = near(axis, step)
        return (lax.rem(at[2], 2), lax.div(at[2], 2) * 32 + at[0] * 8 + at[1] * 2 + core)

    partner = (e, t + 1 - 2 * core)
    peers = [[device(a, step) for step in STEPS] for a in range(3)]

    barrier = pltpu.get_barrier_semaphore()
    for d in [partner] + peers[0] + peers[1] + peers[2]:
        pl.semaphore_signal(barrier, inc=1, device_id=d, device_id_type=MESH)

    here = (pos[2], pos[1], pos[0], core)
    mine = x_all.at[(core, *here)]
    local = []

    def load(src, dst, sem):
        c = pltpu.make_async_copy(src, dst, sem)
        c.start()
        return c

    local.append(load(ids, idv, lsem.at[2, 0]))
    local.append(load(gts, gtv, lsem.at[2, 1]))
    for h, ref in enumerate((mine, st)):
        half = (core, other)[h]
        for i, (src, dst, n) in enumerate(((0, 0, PART), (PART, PART + GATE, 2 * PART))):
            local.append(load(tok.at[:, pl.ds(pl.multiple_of(half * HALF + src, PART), n)],
                              ref.at[:, pl.ds(dst, n)], lsem.at[h, i]))
    weights = [load(src, dst, wsem.at[i]) for i, (src, dst) in enumerate(((wg, wgs), (wu, wus), (wd, wds)))]

    local[0].wait()
    local[1].wait()
    lane = lax.broadcasted_iota(jnp.int32, (4, GATE), 1)
    row = lax.broadcasted_iota(jnp.int32, (4, GATE), 0)
    table = jnp.zeros((4, GATE), F32)
    gvals = gtv[...].astype(F32)
    for j in range(2):
        for r in range(4):
            hit = (row == r) & (lane == idv[j:j + 1, r:r + 1])
            table += jnp.where(hit, gvals[j:j + 1, r:r + 1], 0.0)
    mine[:, pl.ds(PART, GATE)] = table.astype(BF)
    st[:, pl.ds(PART, GATE)] = table.astype(BF)

    for c in local[2:]:
        c.wait()
    pl.semaphore_wait(barrier, 10)

    sent = []

    def send(src, dst, ssem, rsem, dev):
        c = pltpu.make_async_remote_copy(src_ref=src, dst_ref=dst, send_sem=ssem, recv_sem=rsem,
                                         device_id=dev, device_id_type=MESH)
        c.start()
        sent.append(c)
        return c

    c = send(st, x_all.at[(other, *here)], s0, r0, partner)
    acc[...] = jnp.zeros_like(acc)
    c.wait_recv()
    every = slice(None)

    def spot(o, q3, q2, q1=every):
        at = dict(zip(ORDER[o], (q1, q2, q3)))
        return (at[2], at[1], at[0])

    def block(o, q3, q2, q1, cols):
        return x_all.at[(core, *spot(o, q3, q2, q1), every, every, pl.ds(*cols))]

    first, second, third = {}, {}, {}
    for o in range(3):
        a1, a2, a3 = ORDER[o]
        ref = block(o, pos[a3], pos[a2], pos[a1], WHOLE[o])
        for i in range(3):
            first[o, i] = send(ref, ref, a1s.at[o, i], a1r.at[o, i], peers[a1][i])

    def direct(o, j):
        a1, a2, a3 = ORDER[o]
        q2 = near(a2, (0, -1, 1, 2)[j])
        for k, to, cut in ((0, 0, 0), (2, 1, 1), (1, 0, 1), (3, 1, 0)):
            ref = block(o, pos[a3], q2, every, CUT[o][cut])
            third[o, j, k] = send(ref, ref, a3s.at[o, j, k], a3r.at[o, j, k], peers[a3][to])

    def relay(o, j):
        a1, a2, a3 = ORDER[o]
        q2 = near(a2, (0, -1, 1, 2)[j])
        for k, to, cut in ((0, 0, 0), (2, 1, 1)):
            third[o, j, k].wait_recv()
            ref = block(o, near(a3, (-1, 1)[to]), q2, every, CUT[o][cut])
            third[o, j, 4 + to] = send(ref, ref, a3s.at[o, j, 4 + to], a3r.at[o, j, 4 + to], peers[a3][to])

    passed = {}

    def hand(o, j, step):
        ref = block(o, near(ORDER[o][2], step), every, every, WHOLE[o])
        passed[o, j] = send(ref, ref, fs.at[o, j], fr.at[o, j], partner)

    def project(h, o, steps):
        n = len(steps) * 128
        for i, step in enumerate(steps):
            xs[i * 128:(i + 1) * 128, :] = x_all[
                (h, *spot(o, near(ORDER[o][2], step), every), every, every, pl.ds(START[o], PART))
            ].reshape(128, PART)

        def one(k, _):
            for m, w in ((0, wgs), (1, wus)):
                r = jnp.dot(xs[0:n, :], w[k, h * 3 + o], preferred_element_type=F32)
                for i, step in enumerate(steps):
                    at = (k, m, *spot(o, near(ORDER[o][2], step), every))
                    acc[at] = acc[at] + r[i * 128:(i + 1) * 128].reshape(4, 4, 8, 256)
            return 0

        lax.fori_loop(0, 2, one, 0)

    for o in range(3):
        a1, a2, a3 = ORDER[o]
        for i in range(3):
            first[o, i].wait_recv()
        ref = block(o, pos[a3], pos[a2], every, WHOLE[o])
        for i in range(3):
            second[o, i] = send(ref, ref, a2s.at[o, i], a2r.at[o, i], peers[a2][i])
        direct(o, 0)
    for i in range(3):
        for o in range(3):
            second[o, i].wait_recv()
            direct(o, i + 1)
            if i == 2:
                hand(o, 0, 0)
    for o in range(3):
        relay(o, 0)
    weights[0].wait()
    weights[1].wait()
    for j in range(3):
        project(core, j, (0,))
        for o in range(3):
            relay(o, j + 1)
    for o in range(3):
        for j in range(4):
            third[o, j, 1].wait_recv()
            third[o, j, 3].wait_recv()
        hand(o, 1, -1)
        hand(o, 2, 1)
    for o in range(3):
        project(core, o, (-1, 1))
    for o in range(3):
        for j in range(4):
            third[o, j, 4].wait_recv()
            third[o, j, 5].wait_recv()
        hand(o, 3, 2)
    for o in range(3):
        project(core, o, (2,))
    for o in range(3):
        for j in range(4):
            passed[o, j].wait_recv()
        project(other, o, (0, 1, -1, 2))

    table = x_all[core, :, :, :, :, :, pl.ds(PART, GATE)].reshape(512, GATE).astype(F32)
    lane = lax.broadcasted_iota(jnp.int32, (512, GATE), 1)
    for k in range(2):
        g = jnp.sum(jnp.where(lane == 2 * e + k, table, 0.0), axis=1, keepdims=True)
        v = acc[k, 0].reshape(512, 256)
        u = acc[k, 1].reshape(512, 256)
        hid[:, k * 256:(k + 1) * 256] = (v / (1.0 + jnp.exp(-v)) * u * g).astype(BF)

    weights[2].wait()

    def down(h, o, n):
        cols = pl.multiple_of(h * HALF + o * PART + n * 256, 256)
        r = jnp.dot(hid[...], wds[:, pl.ds(cols, 256)], preferred_element_type=F32)
        return pl.ds(pl.multiple_of(n * 256, 256), 256), r.reshape(4, 4, 4, 8, 256)

    LOW, HIGH = pl.ds(0, 512), pl.ds(512, 512)
    pair = {}
    for o in range(3):
        def give(n, _):
            at, r = down(other, o, n)
            sp[o, :, :, :, :, at] = r.astype(BF)
            return 0

        for u, cols in enumerate((LOW, HIGH)):
            lax.fori_loop(2 * u, 2 * u + 2, give, 0)
            at = (o, every, every, every, every, cols)
            pair[o, u] = send(sp.at[at], rp.at[at], ps.at[o, u], pr.at[o, u], partner)

    AWAY = (2, 1, -1, 0)
    moves = {}

    def begin(o):
        a1, a2, a3 = ORDER[o]
        for ks in (((0, 2, LOW, 0), (1, 2, HIGH, 1)), ((2, 1, HIGH, 0), (3, -1, LOW, 1))):
            for j in range(4):
                for k, step, cols, to in ks:
                    src = own16.at[(o, *spot(o, near(a3, step), near(a2, AWAY[j])), every, cols)]
                    moves[o, j, k] = send(src, ra.at[o, j, k], b1s.at[o, j, k], b1r.at[o, j, k], peers[a3][to])

    def merge(o, j):
        a1, a2, a3 = ORDER[o]
        for k, step, cols, to in ((0, 1, LOW, 0), (1, -1, HIGH, 1)):
            moves[o, j, k].wait_recv()
            at = (o, *spot(o, near(a3, step), near(a2, AWAY[j])), every, cols)
            ma[o, j, k] = (own[at] + ra[o, j, k].astype(F32)).astype(BF)
            moves[o, j, 4 + k] = send(ma.at[o, j, k], ra.at[o, j, 4 + k], b1s.at[o, j, 4 + k],
                                      b1r.at[o, j, 4 + k], peers[a3][to])

    turn = {}

    def final(o, j):
        a1, a2, a3 = ORDER[o]
        for cols, ks in ((LOW, (3, 4)), (HIGH, (2, 5))):
            r = own[(o, *spot(o, pos[a3], near(a2, AWAY[j])), every, cols)]
            for k in ks:
                moves[o, j, k].wait_recv()
                r = r + ra[o, j, k].astype(F32)
            if j < 3:
                tb16[o, j, :, :, cols] = r.astype(BF)
            else:
                ta[o, :, :, cols] = r
        if j < 3:
            turn[o, j] = send(tb16.at[o, j], rb.at[o, j], b2s.at[o, j], b2r.at[o, j], peers[a2][(2, 0, 1)[j]])

    for o in range(3):
        def keep(n, _):
            at, r = down(core, o, n)
            r = r + rp[o, :, :, :, :, at].astype(F32)
            own[o, :, :, :, :, at] = r
            own16[o, :, :, :, :, at] = r.astype(BF)
            return 0

        for u in range(2):
            pair[o, u].wait_recv()
            lax.fori_loop(2 * u, 2 * u + 2, keep, 0)
        begin(o)
    for j in range(4):
        for o in range(3):
            merge(o, j)
            if j > 0:
                final(o, j - 1)
    last = {}
    for o in range(3):
        final(o, 3)
    for o in range(3):
        a1, a2, a3 = ORDER[o]
        r = ta[o]
        for j in range(3):
            turn[o, j].wait_recv()
            r = r + rb[o, j].astype(F32)
        tb[o] = r
        for i in range(3):
            last[o, i] = send(tb.at[o, near(a1, STEPS[i])], rc.at[o, i], b3s.at[o, i], b3r.at[o, i], peers[a1][i])
    for o in range(3):
        r = tb[o, pos[ORDER[o][0]]]
        for i in range(3):
            last[o, i].wait_recv()
            r = r + rc[o, i]
        sd[:, pl.ds(o * PART, PART)] = jnp.where(core == 0, r[4:8], r[0:4])
        to = pl.multiple_of(core * HALF + o * PART, PART)
        out[:, pl.ds(to, PART)] = jnp.where(core == 0, r[0:4], r[4:8]).astype(BF)
    c = send(sd, rd, ds, dr, partner)
    c.wait_recv()
    out[:, pl.ds(pl.multiple_of(other * HALF, HALF), HALF)] = rd[...].astype(BF)
    for c in sent:
        c.wait_send()


def shards(tokens, gate_weights, expert_ids, w_gate, w_up, w_down):
    anyspace = pl.BlockSpec(memory_space=pl.ANY)
    vmem = pl.BlockSpec(memory_space=pltpu.VMEM)
    dma = pltpu.SemaphoreType.DMA
    return pl.pallas_call(
        kernel,
        out_shape=jax.ShapeDtypeStruct((4, 2 * HALF), BF),
        in_specs=[anyspace] * 6,
        out_specs=vmem,
        scratch_shapes=[
            pltpu.VMEM((2, 4, 4, 4, 2, 4, WIDE), BF),
            pltpu.VMEM((4, WIDE), BF),
            pltpu.VMEM((2, 4), jnp.int32),
            pltpu.VMEM((2, 4), BF),
            pltpu.VMEM((2, 6, PART, 256), BF),
            pltpu.VMEM((2, 6, PART, 256), BF),
            pltpu.VMEM((512, 2 * HALF), BF),
            pltpu.VMEM((512, PART), BF),
            pltpu.VMEM((2, 2, 4, 4, 4, 8, 256), F32),
            pltpu.VMEM((512, 512), BF),
            pltpu.VMEM((3, 4, 4, 4, 8, PART), F32),
            pltpu.VMEM((3, 4, 4, 4, 8, PART), BF),
            pltpu.VMEM((3, 4, 4, 4, 8, PART), BF),
            pltpu.VMEM((3, 4, 4, 4, 8, PART), BF),
            pltpu.VMEM((3, 4, 2, 4, 8, 512), BF),
            pltpu.VMEM((3, 4, 6, 4, 8, 512), BF),
            pltpu.VMEM((3, 4, 8, PART), F32),
            pltpu.VMEM((3, 3, 4, 8, PART), BF),
            pltpu.VMEM((3, 3, 4, 8, PART), BF),
            pltpu.VMEM((3, 4, 8, PART), F32),
            pltpu.VMEM((3, 3, 8, PART), F32),
            pltpu.VMEM((4, HALF), F32),
            pltpu.VMEM((4, HALF), F32),
            dma((3, 2)), dma((3,)), dma, dma, dma((3, 3)), dma((3, 3)), dma((3, 3)), dma((3, 3)),
            dma((3, 4, 6)), dma((3, 4, 6)), dma((3, 4)), dma((3, 4)), dma((3, 2)), dma((3, 2)),
            dma((3, 4, 6)), dma((3, 4, 6)), dma((3, 3)), dma((3, 3)), dma((3, 3)), dma((3, 3)), dma, dma,
        ],
        compiler_params=pltpu.CompilerParams(
            collective_id=0, has_side_effects=True, vmem_limit_bytes=67043328),
        name="moe",
    )(tokens, expert_ids.T, gate_weights.T, w_gate.reshape(2, 6, PART, 256), w_up.reshape(2, 6, PART, 256),
      w_down.reshape(512, 2 * HALF))


def solution(mesh):
    rows = P(("expert", "tensor"), None)
    return jax.shard_map(
        shards, mesh=mesh,
        in_specs=(rows, rows, rows, P("expert", None, "tensor"), P("expert", None, "tensor"),
                  P("expert", "tensor", None)),
        out_specs=rows, check_vma=False)
```
